32 devices in a mesh: grp: 2 (over x), row: 16 (over z, y, core).
Axes of the slice: x: 2, y: 2, z: 4, core: 2. Of those that a mesh axis runs over, the one named last changes fastest.
Arguments:
- inputs: bfloat16 [8192, 8192], P(('grp', 'row')), parts along dimension 0, may hold values from -6 to 6
- out_grads: bfloat16 [8192, 8192], P(('grp', 'row')), parts along dimension 0, may hold values from -6 to 6
- proj_in: bfloat16 [8192, 64], replicated, may hold values from -0.0625 to 0.0625
- proj_out: bfloat16 [8192, 64], replicated, may hold values from -0.0625 to 0.0625
- example_ids: int32 [8192], P(('grp', 'row')), parts along dimension 0, may hold values from 0 to 7, as said below
Outputs:
- gram: float32 [256, 128], P(('grp', 'row')), parts along dimension 0
The draws below stay inside these ranges and needn't reach their ends.
There are 2 independent parts, one for each index of `grp`. The reference program is written for one: setup_inputs(seed, part) draws one part's arguments, and reference() takes and returns one part's arrays. A program takes and returns all parts, laid end to end along the dimension named above; an argument that names none is the same for every part. Nothing has to cross between parts.
Inputs may be any that keep to these rules, and one draw needn't show every extreme that they name: `example_ids`: within each aligned block of 256 tokens every value 0 to 7 appears exactly 32 times, in an order drawn from the seed.
All inputs are finite; a program needn't handle non-finite values.
Results may differ from the reference program's by a relative error of at most 0.0025.
Values may be sent and summed in bfloat16 or wider, within the bound.
No kernel may reach another device: no remote copies, remote signals or barrier semaphores. Data moves between devices by JAX's collectives and lax.ppermute only.
A program may use at most 64 MiB of HBM per device.

```python
import math
import jax
import jax.numpy as jnp

D = 8192
RANK = 64
TPE = 32
EX_DEV = 8
TOK_DEV = 256
EXAMPLES = 128
TOKENS = 4096


def draw_example_ids(key, part):
    blocks = TOKENS // TOK_DEV
    pattern = jnp.arange(TOK_DEV, dtype=jnp.int32) // TPE
    splits = jax.random.split(jax.random.fold_in(key, 11), blocks)
    shuffled = jax.vmap(lambda subkey: jax.random.permutation(subkey, pattern))(splits)
    return shuffled.reshape(TOKENS).astype(jnp.int32)


def shard_levels(stream_key, shape, pieces, low, top_value):
    level, own = 1.0, jax.random.fold_in(stream_key, 6)
    for dim, parts in pieces:
        heights = jnp.exp(jax.random.uniform(jax.random.fold_in(own, dim), (parts,), jnp.float32, low / len(pieces), top_value / len(pieces)))
        level = level * jnp.repeat(heights, shape[dim] // parts).reshape([-1 if axis == dim else 1 for axis in range(len(shape))])
    return level


def bell_draw(key, dims, spread, bound, cuts=(), kind=jnp.bfloat16):
    drawn = spread * jax.random.normal(key, dims, jnp.float32)
    if cuts:
        drawn = drawn * shard_levels(key, dims, cuts, -0.22, 0.18)
    return jnp.clip(drawn, -bound, bound).astype(kind)


def setup_inputs(seed: int = 0, part: int = 0) -> dict:
    arg_keys = jax.random.split(jax.random.key(seed), 6)
    own_keys = jax.random.split(jax.random.fold_in(arg_keys[5], part), 6)
    inputs = bell_draw(own_keys[0], (TOKENS, D), 1.0, 6.0, ((0, 16),))
    out_grads = bell_draw(own_keys[1], (TOKENS, D), 1.0, 6.0, ((0, 16),))
    proj_in = bell_draw(arg_keys[2], (D, RANK), D ** -0.5, 0.0625)
    proj_out = bell_draw(arg_keys[3], (D, RANK), D ** -0.5, 0.0625)
    example_ids = draw_example_ids(jax.random.fold_in(jax.random.fold_in(arg_keys[5], part), 71), part)
    return dict(inputs=inputs, out_grads=out_grads, proj_in=proj_in, proj_out=proj_out, example_ids=example_ids)


def reference(inputs, out_grads, proj_in, proj_out, example_ids):
    xproj = jnp.dot(inputs, proj_in, preferred_element_type=jnp.float32).astype(jnp.bfloat16)
    gproj = jnp.dot(out_grads, proj_out, preferred_element_type=jnp.float32).astype(jnp.bfloat16)
    blocks = TOKENS // TOK_DEV
    block_ids = example_ids.reshape(blocks, TOK_DEV)
    onehot = (block_ids[:, None, :] == jnp.arange(EX_DEV, dtype=jnp.int32)[None, :, None]).astype(jnp.float32)
    grad_blocks = gproj.astype(jnp.float32).reshape(blocks, TOK_DEV, RANK)
    input_blocks = xproj.astype(jnp.float32).reshape(blocks, TOK_DEV, RANK)
    weighted = onehot[:, :, :, None] * grad_blocks[:, None, :, :]
    outer = jnp.einsum('betp,btq->bepq', weighted, input_blocks)
    scale_factor = 1.0 / math.sqrt(TPE)
    features = (outer.reshape(EXAMPLES, RANK * RANK) * scale_factor).astype(jnp.bfloat16)
    gram = jnp.dot(features, features.T, preferred_element_type=jnp.float32) / RANK
    return gram
```

```python
import functools
import math

import jax
import jax.numpy as jnp
from jax import lax
from jax.experimental import pallas as pl
from jax.experimental.pallas import tpu as pltpu
from jax.sharding import PartitionSpec as P

RANK = 64
TPE = 32
EX_DEV = 8
CHUNKS = 4
PACK = 16
LANES = 128
NT = (((1,), (1,)), ((), ()))
VM = pl.BlockSpec(memory_space=pltpu.VMEM)
ANY = pl.BlockSpec(memory_space=pl.ANY)


def features_kernel(ids_ref, x_hbm, g_hbm, pi_hbm, po_hbm, f_ref, xv, gv, piv, pov, ax, ag, sems):
    tokens, depth = x_hbm.shape
    rank = pi_hbm.shape[0]
    half = rank // 2
    step = depth // CHUNKS
    sides = ((x_hbm, pi_hbm, xv, piv, ax), (g_hbm, po_hbm, gv, pov, ag))

    def copies(side, c):
        act_hbm, proj_hbm, act, proj, _ = sides[side]
        cols = pl.ds(pl.multiple_of(c * step, step), step)
        return (
            pltpu.make_async_copy(proj_hbm.at[:, cols], proj.at[:, cols], sems.at[2 * side, c]),
            pltpu.make_async_copy(act_hbm.at[:, cols], act.at[:, cols], sems.at[2 * side + 1, c]),
        )

    for side in (0, 1):
        for c in range(CHUNKS):
            for copy in copies(side, c):
                copy.start()
    ax[...] = jnp.zeros_like(ax)
    ag[...] = jnp.zeros_like(ag)
    for side in (0, 1):
        _, _, act, proj, acc = sides[side]

        @pl.loop(0, CHUNKS)
        def _(c, side=side, act=act, proj=proj, acc=acc):
            for copy in copies(side, c):
                copy.wait()
            cols = pl.ds(pl.multiple_of(c * step, step), step)
            acc[...] += lax.dot_general(
                proj[:, cols], act[:, cols], NT, preferred_element_type=jnp.float32
            )

    gt = ag[...].astype(jnp.bfloat16).astype(jnp.float32)
    xt = ax[...].astype(jnp.bfloat16)
    mask = ids_ref[...] == lax.broadcasted_iota(jnp.int32, (EX_DEV, tokens), 0)
    mask = mask.astype(jnp.float32)
    rows = [
        jnp.concatenate([gt[p : p + 1] * mask, gt[p + half : p + half + 1] * mask], axis=1)
        for p in range(half)
    ]
    left = jnp.concatenate(rows, axis=0).astype(jnp.bfloat16)
    zero = jnp.zeros_like(xt)
    right = jnp.concatenate(
        [jnp.concatenate([xt, zero], axis=1), jnp.concatenate([zero, xt], axis=1)], axis=0
    )
    outer = lax.dot_general(left, right, NT, preferred_element_type=jnp.float32)
    f_ref[...] = (outer * (1.0 / math.sqrt(TPE))).astype(jnp.bfloat16).reshape(f_ref.shape)


def features_of(inputs, out_grads, proj_in, proj_out, example_ids):
    tokens, depth = inputs.shape
    rank = proj_in.shape[1]
    return pl.pallas_call(
        features_kernel,
        out_shape=pltpu.VMEM((rank * EX_DEV // 2 // PACK, PACK, 2 * rank), jnp.bfloat16),
        in_specs=[VM, ANY, ANY, ANY, ANY],
        out_specs=VM,
        scratch_shapes=[
            pltpu.VMEM((tokens, depth), jnp.bfloat16),
            pltpu.VMEM((tokens, depth), jnp.bfloat16),
            pltpu.VMEM((rank, depth), jnp.bfloat16),
            pltpu.VMEM((rank, depth), jnp.bfloat16),
            pltpu.VMEM((rank, tokens), jnp.float32),
            pltpu.VMEM((rank, tokens), jnp.float32),
            pltpu.SemaphoreType.DMA((4, CHUNKS)),
        ],
        name="features",
    )(example_ids.reshape(1, tokens), inputs, out_grads, proj_in.T, proj_out.T)


def near(x):
    return pltpu.with_memory_space_constraint(x, pltpu.VMEM)


def gram_kernel(f_ref, fp_ref, cols_ref, *refs):
    before, after = refs[: len(refs) - 2], refs[len(refs) - 2 :]
    chunks, width, _ = cols_ref.shape
    acc = jnp.zeros((2 * PACK, width), jnp.float32)
    for q in range(0, chunks, 2):
        left = jnp.concatenate(
            [
                jnp.concatenate([f_ref[q], f_ref[q + 1]], axis=1),
                jnp.concatenate([fp_ref[q], fp_ref[q + 1]], axis=1),
            ],
            axis=0,
        )
        right = jnp.concatenate([cols_ref[q], cols_ref[q + 1]], axis=1)
        acc += lax.dot_general(left, right, NT, preferred_element_type=jnp.float32)
    for side in (0, 1):
        even = acc[side * PACK : side * PACK + EX_DEV]
        odd = acc[side * PACK + EX_DEV : (side + 1) * PACK]
        odd = jnp.concatenate([odd[:, EX_DEV:], odd[:, :EX_DEV]], axis=1)
        both = (even + odd) * (1.0 / RANK)
        if before:
            both = jnp.concatenate([before[side][...], both], axis=1)
        after[side][...] = both


def gram_of(f, fp, cols, before=()):
    chunks, width, lanes = cols.shape
    n_cols = width + (before[0].shape[1] if before else 0)
    return pl.pallas_call(
        gram_kernel,
        out_shape=[pltpu.VMEM((EX_DEV, n_cols), jnp.float32)] * 2,
        in_specs=[VM] * (3 + len(before)),
        out_specs=[VM, VM],
        cost_estimate=pl.CostEstimate(
            flops=4 * PACK * width * chunks * lanes,
            bytes_accessed=2 * chunks * lanes * (width + 2 * PACK),
            transcendentals=0,
        ),
        name="gram",
    )(*map(near, (f, fp, cols, *before)))


def place_kernel(orders, own_ref, other_ref, out_ref):
    me = lax.axis_index("row")
    width, n_cols = own_ref.shape[1], out_ref.shape[1]
    col = lax.broadcasted_iota(jnp.int32, (width, n_cols), 1)
    row = lax.broadcasted_iota(jnp.int32, (width, n_cols), 0)
    offset = (col // EX_DEV) ^ me

    def source(core):
        pos = jnp.zeros_like(col)
        for j, (bit0, bit1) in enumerate(zip(*orders)):
            bit = jnp.where(core == 0, bit0, bit1)
            pos += jnp.where((offset & bit) != 0, 1 << j, 0)
        return pos * PACK + col % EX_DEV

    core = me & 1
    mine = (offset & 1) == 0
    pick_own = (mine & (row == source(core))).astype(jnp.float32)
    pick_other = (~mine & (row == source(1 - core))).astype(jnp.float32)
    dot = functools.partial(
        jnp.dot, precision=lax.Precision.HIGHEST, preferred_element_type=jnp.float32
    )
    out_ref[...] = dot(own_ref[...], pick_own) + dot(other_ref[...], pick_other)


def shards(n, inputs, out_grads, proj_in, proj_out, example_ids):
    bits = [1 << b for b in range(n.bit_length() - 2, 0, -1)]
    orders = (bits, bits[:-2] + bits[-2:][::-1])
    core = [(i, i ^ 1) for i in range(n)]
    f = features_of(inputs, out_grads, proj_in, proj_out, example_ids)
    fp = lax.ppermute(f, "row", core)
    held = f
    for j in range(len(bits)):
        perm = [(i, i ^ orders[i & 1][j]) for i in range(n)]
        came = lax.ppermute(held, "row", perm)
        if j < len(bits) - 1:
            held = jnp.concatenate([held, came], axis=1)
    own, other = gram_of(f, fp, came, gram_of(f, fp, held))
    got = lax.ppermute(other, "row", core)
    return pl.pallas_call(
        functools.partial(place_kernel, orders),
        out_shape=jax.ShapeDtypeStruct((EX_DEV, n * EX_DEV), jnp.float32),
        in_specs=[VM, VM],
        out_specs=VM,
        name="place",
    )(near(own), near(got))


def solution(mesh):
    in_specs = (P(("grp", "row"), None), P(("grp", "row"), None), P(), P(), P(("grp", "row")))
    out_specs = P(("grp", "row"), None)
    body = functools.partial(shards, mesh.shape["row"])
    return jax.shard_map(body, mesh=mesh, in_specs=in_specs, out_specs=out_specs, check_vma=False)
```

```python
import functools
import math

import jax
import jax.numpy as jnp
from jax import lax
from jax.experimental import pallas as pl
from jax.experimental.pallas import tpu as pltpu
from jax.sharding import PartitionSpec as P

RANK = 64
TPE = 32
EX_DEV = 8
CHUNKS = 4
PACK = 16
LANES = 128
NT = (((1,), (1,)), ((), ()))
VM = pl.BlockSpec(memory_space=pltpu.VMEM)
ANY = pl.BlockSpec(memory_space=pl.ANY)


def features_kernel(ids_ref, x_hbm, g_hbm, pi_hbm, po_hbm, f_ref, xv, gv, piv, pov, ax, ag, sems):
    tokens, depth = x_hbm.shape
    rank = pi_hbm.shape[0]
    half = rank // 2
    step = depth // CHUNKS
    sides = ((x_hbm, pi_hbm, xv, piv, ax), (g_hbm, po_hbm, gv, pov, ag))

    def copies(side, c):
        act_hbm, proj_hbm, act, proj, _ = sides[side]
        cols = pl.ds(pl.multiple_of(c * step, step), step)
        return (
            pltpu.make_async_copy(proj_hbm.at[:, cols], proj.at[:, cols], sems.at[2 * side, c]),
            pltpu.make_async_copy(act_hbm.at[:, cols], act.at[:, cols], sems.at[2 * side + 1, c]),
        )

    for side in (0, 1):
        for c in range(CHUNKS):
            for copy in copies(side, c):
                copy.start()
    ax[...] = jnp.zeros_like(ax)
    ag[...] = jnp.zeros_like(ag)
    for side in (0, 1):
        _, _, act, proj, acc = sides[side]

        @pl.loop(0, CHUNKS)
        def _(c, side=side, act=act, proj=proj, acc=acc):
            for copy in copies(side, c):
                copy.wait()
            cols = pl.ds(pl.multiple_of(c * step, step), step)
            acc[...] += lax.dot_general(
                proj[:, cols], act[:, cols], NT, preferred_element_type=jnp.float32
            )

    gt = ag[...].astype(jnp.bfloat16).astype(jnp.float32)
    xt = ax[...].astype(jnp.bfloat16)
    mask = ids_ref[...] == lax.broadcasted_iota(jnp.int32, (EX_DEV, tokens), 0)
    mask = mask.astype(jnp.float32)
    rows = [
        jnp.concatenate([gt[p : p + 1] * mask, gt[p + half : p + half + 1] * mask], axis=1)
        for p in range(half)
    ]
    left = jnp.concatenate(rows, axis=0).astype(jnp.bfloat16)
    zero = jnp.zeros_like(xt)
    right = jnp.concatenate(
        [jnp.concatenate([xt, zero], axis=1), jnp.concatenate([zero, xt], axis=1)], axis=0
    )
    outer = lax.dot_general(left, right, NT, preferred_element_type=jnp.float32)
    f_ref[...] = (outer * (1.0 / math.sqrt(TPE))).astype(jnp.bfloat16).reshape(f_ref.shape)


def features_of(inputs, out_grads, proj_in, proj_out, example_ids):
    tokens, depth = inputs.shape
    rank = proj_in.shape[1]
    return pl.pallas_call(
        features_kernel,
        out_shape=pltpu.VMEM((rank * EX_DEV // 2 // PACK, PACK, 2 * rank), jnp.bfloat16),
        in_specs=[VM, ANY, ANY, ANY, ANY],
        out_specs=VM,
        scratch_shapes=[
            pltpu.VMEM((tokens, depth), jnp.bfloat16),
            pltpu.VMEM((tokens, depth), jnp.bfloat16),
            pltpu.VMEM((rank, depth), jnp.bfloat16),
            pltpu.VMEM((rank, depth), jnp.bfloat16),
            pltpu.VMEM((rank, tokens), jnp.float32),
            pltpu.VMEM((rank, tokens), jnp.float32),
            pltpu.SemaphoreType.DMA((4, CHUNKS)),
        ],
        name="features",
    )(example_ids.reshape(1, tokens), inputs, out_grads, proj_in.T, proj_out.T)


def near(x):
    return pltpu.with_memory_space_constraint(x, pltpu.VMEM)


def gram_kernel(n_cols, f_ref, fp_ref, *refs):
    cols, before, after = refs[:n_cols], refs[n_cols:-2], refs[-2:]
    chunks = f_ref.shape[0]

    def wide(ref, q):
        return jnp.concatenate([ref[q], ref[q + 1]], axis=1)

    acc = jnp.zeros((2 * PACK, sum(ref.shape[1] for ref in cols)), jnp.float32)
    for q in range(0, chunks, 2):
        left = jnp.concatenate([wide(f_ref, q), wide(fp_ref, q)], axis=0)
        right = jnp.concatenate([wide(ref, q) for ref in cols], axis=0)
        acc += lax.dot_general(left, right, NT, preferred_element_type=jnp.float32)
    for side in (0, 1):
        even = acc[side * PACK : side * PACK + EX_DEV]
        odd = acc[side * PACK + EX_DEV : (side + 1) * PACK]
        odd = jnp.concatenate([odd[:, EX_DEV:], odd[:, :EX_DEV]], axis=1)
        both = (even + odd) * (1.0 / RANK)
        if before:
            both = jnp.concatenate([before[side][...], both], axis=1)
        after[side][...] = both


def gram_of(f, fp, cols, before=()):
    chunks, _, lanes = f.shape
    width = sum(c.shape[1] for c in cols)
    n_cols = width + (before[0].shape[1] if before else 0)
    return pl.pallas_call(
        functools.partial(gram_kernel, len(cols)),
        out_shape=[pltpu.VMEM((EX_DEV, n_cols), jnp.float32)] * 2,
        in_specs=[VM] * (2 + len(cols) + len(before)),
        out_specs=[VM, VM],
        cost_estimate=pl.CostEstimate(
            flops=4 * PACK * width * chunks * lanes,
            bytes_accessed=2 * chunks * lanes * (width + 2 * PACK),
            transcendentals=0,
        ),
        name="gram",
    )(*map(near, (f, fp, *cols, *before)))


def place_kernel(orders, own_ref, other_ref, out_ref):
    me = lax.axis_index("row")
    width, n_cols = own_ref.shape[1], out_ref.shape[1]
    col = lax.broadcasted_iota(jnp.int32, (width, n_cols), 1)
    row = lax.broadcasted_iota(jnp.int32, (width, n_cols), 0)
    offset = (col // EX_DEV) ^ me

    def source(core):
        pos = jnp.zeros_like(col)
        for j, (bit0, bit1) in enumerate(zip(*orders)):
            bit = jnp.where(core == 0, bit0, bit1)
            pos += jnp.where((offset & bit) != 0, 1 << j, 0)
        return pos * PACK + col % EX_DEV

    core = me & 1
    mine = (offset & 1) == 0
    pick_own = (mine & (row == source(core))).astype(jnp.float32)
    pick_other = (~mine & (row == source(1 - core))).astype(jnp.float32)
    dot = functools.partial(
        jnp.dot, precision=lax.Precision.HIGHEST, preferred_element_type=jnp.float32
    )
    out_ref[...] = dot(own_ref[...], pick_own) + dot(other_ref[...], pick_other)


def shards(n, inputs, out_grads, proj_in, proj_out, example_ids):
    bits = [1 << b for b in range(n.bit_length() - 2, 0, -1)]
    orders = (bits[:-2] + bits[-2:][::-1], bits[-1:] + bits[:-1])
    core = [(i, i ^ 1) for i in range(n)]
    f = features_of(inputs, out_grads, proj_in, proj_out, example_ids)
    fp = lax.ppermute(f, "row", core)

    def swap(x, j):
        return lax.ppermute(x, "row", [(i, i ^ orders[i & 1][j]) for i in range(n)])

    last = len(bits) - 1
    held = f
    for j in range(last - 1):
        held = jnp.concatenate([held, swap(held, j)], axis=1)
    came = swap(held, last - 1)
    first = swap(held, last)
    second = swap(came, last)
    own, other = gram_of(f, fp, [first, second], gram_of(f, fp, [held, came]))
    got = lax.ppermute(other, "row", core)
    return pl.pallas_call(
        functools.partial(place_kernel, orders),
        out_shape=jax.ShapeDtypeStruct((EX_DEV, n * EX_DEV), jnp.float32),
        in_specs=[VM, VM],
        out_specs=VM,
        name="place",
    )(near(own), near(got))


def solution(mesh):
    in_specs = (P(("grp", "row"), None), P(("grp", "row"), None), P(), P(), P(("grp", "row")))
    out_specs = P(("grp", "row"), None)
    body = functools.partial(shards, mesh.shape["row"])
    return jax.shard_map(body, mesh=mesh, in_specs=in_specs, out_specs=out_specs, check_vma=False)
```
